32 devices in a mesh: dp: 16 (over z, y, core), seq: 2 (over x).
Axes of the slice: x: 2, y: 2, z: 4, core: 2. Of those that a mesh axis runs over, the one named last changes fastest.
Arguments:
- decoder_in: bfloat16 [8192, 768], P(('dp', 'seq')), may hold values from -6 to 6
- encoder_out: bfloat16 [8192, 768], P(('dp', 'seq')), may hold values from -6 to 6
- decoder_segments: int32 [16, 512], P('dp'), may hold values from 0 to 3, as said below
- encoder_segments: int32 [16, 512], P('dp'), may hold values from 0 to 3, as said below
- rel_buckets: int32 [512], replicated, may hold values from 0 to 31, as said below
- self_gain: float32 [768], replicated, may hold values from 0.5 to 1.5
- self_query: bfloat16 [768, 768], P(None, 'seq'), may hold values from -0.109375 to 0.109375
- self_key: bfloat16 [768, 768], P(None, 'seq'), may hold values from -0.109375 to 0.109375
- self_value: bfloat16 [768, 768], P(None, 'seq'), may hold values from -0.21875 to 0.21875
- self_output: bfloat16 [768, 768], P('seq'), may hold values from -0.875 to 0.875
- bias_table: float32 [32, 12], P(None, 'seq'), may hold values from -4 to 4
- cross_gain: float32 [768], replicated, may hold values from 0.5 to 1.5
- cross_query: bfloat16 [768, 768], P(None, 'seq'), may hold values from -0.109375 to 0.109375
- cross_key: bfloat16 [768, 768], P(None, 'seq'), may hold values from -0.109375 to 0.109375
- cross_value: bfloat16 [768, 768], P(None, 'seq'), may hold values from -0.21875 to 0.21875
- cross_output: bfloat16 [768, 768], P('seq'), may hold values from -0.875 to 0.875
- ffn_gain: float32 [768], replicated, may hold values from 0.5 to 1.5
- ffn_gate: bfloat16 [768, 2048], replicated, may hold values from -0.21875 to 0.21875
- ffn_up: bfloat16 [768, 2048], replicated, may hold values from -0.21875 to 0.21875
- ffn_down: bfloat16 [2048, 768], replicated, may hold values from -0.25 to 0.25
- cotangent: bfloat16 [8192, 768], P(('dp', 'seq')), may hold values from -6 to 6
Outputs:
- layer_out: bfloat16 [8192, 768], P(('dp', 'seq'))
- grad_decoder: float32 [8192, 768], P(('dp', 'seq'))
- grad_encoder: float32 [8192, 768], P(('dp', 'seq'))
- grad_self_gain: float32 [768], replicated
- grad_self_query: float32 [768, 768], P('dp', 'seq')
- grad_self_key: float32 [768, 768], P('dp', 'seq')
- grad_self_value: float32 [768, 768], P('dp', 'seq')
- grad_self_output: float32 [768, 768], P('seq', 'dp')
- grad_bias_table: float32 [32, 12], replicated
- grad_cross_gain: float32 [768], replicated
- grad_cross_query: float32 [768, 768], P('dp', 'seq')
- grad_cross_key: float32 [768, 768], P('dp', 'seq')
- grad_cross_value: float32 [768, 768], P('dp', 'seq')
- grad_cross_output: float32 [768, 768], P('seq', 'dp')
- grad_ffn_gain: float32 [768], replicated
- grad_ffn_gate: float32 [768, 2048], P(None, ('dp', 'seq'))
- grad_ffn_up: float32 [768, 2048], P(None, ('dp', 'seq'))
- grad_ffn_down: float32 [2048, 768], P(('dp', 'seq'))
The draws below stay inside these ranges and needn't reach their ends.
Inputs may be any that keep to these rules, and one draw needn't show every extreme that they name: `decoder_segments`: in each row the document numbers never fall along the row, and every number from 0 to 3 occurs in it. `encoder_segments`: in each row the document numbers never fall along the row, and every number from 0 to 3 occurs in it. `rel_buckets`: A general monotone bucketing of the causal distance, not a fixed logarithmic rule: never falls with the distance, is 0 at distance 0, and every bucket occurs.
All inputs are finite; a program needn't handle non-finite values.
Results may differ from the reference program's by a relative error of at most 0.029.
The reference program's roundings to bfloat16 on the way count: a program that leaves them out, or rounds other values in their place, can miss the bound.
Values may be sent and summed in bfloat16 or wider, within the bound.
No kernel may reach another device: no remote copies, remote signals or barrier semaphores. Data moves between devices by JAX's collectives and lax.ppermute only.
A program may use at most 320 MiB of HBM per device.

```python
import jax
import jax.numpy as jnp
from jax import lax

D = 768
H = 12
DH = 64
FF = 2048
NB = 32
LEN = 512
DOCS = 4
ROWS = 16
TOKENS = 8192


def segment_rows(key, rows, length, docs):
    keys = jax.random.split(key, rows)

    def one_row(row_key):
        shuffled = jax.random.permutation(row_key, length - 1).astype(jnp.int32) + 1
        cuts = shuffled[:docs - 1]
        places = jnp.arange(length, dtype=jnp.int32)
        return jnp.sum((places[:, None] >= cuts[None, :]).astype(jnp.int32), axis=1)
    return jax.vmap(one_row)(keys)


def draw_decoder_segments(key, part):
    return segment_rows(jax.random.fold_in(key, 11), ROWS, LEN, DOCS)


def draw_encoder_segments(key, part):
    return segment_rows(jax.random.fold_in(key, 23), ROWS, LEN, DOCS)


def draw_rel_buckets(key, part):
    shuffled = jax.random.permutation(jax.random.fold_in(key, 37), LEN - 1).astype(jnp.int32) + 1
    cuts = shuffled[:NB - 1]
    places = jnp.arange(LEN, dtype=jnp.int32)
    return jnp.sum((places[:, None] >= cuts[None, :]).astype(jnp.int32), axis=1)


def raised(entries, key, source, target, parts, factor):
    def block_of(dim):
        return (jnp.arange(entries.shape[dim]) // (entries.shape[dim] // parts)).reshape((-1,) + (1,) * (entries.ndim - 1 - dim))

    first = jax.random.permutation(key, parts)[block_of(target)]
    far = (block_of(target) + parts // 2) % parts
    return jnp.where((block_of(source) == first) | (block_of(source) == far), factor * entries, entries)


def steps_of(rng, shape, cuts, smallest, top_value):
    def one(axis_at, parts):
        draws = jax.random.uniform(jax.random.fold_in(jax.random.fold_in(rng, 6), axis_at), (parts,), jnp.float32, smallest / len(cuts), top_value / len(cuts))
        return jnp.repeat(jnp.exp(draws), shape[axis_at] // parts).reshape((-1,) + (1,) * (len(shape) - axis_at - 1))

    factor_of = one(*cuts[0])
    for cut in cuts[1:]:
        factor_of = factor_of * one(*cut)
    return factor_of


def scatter_about(own_key, extent, spread, most, cuts=(), kind=jnp.bfloat16):
    array = spread * jax.random.normal(own_key, extent, jnp.float32)
    if cuts:
        array = array * steps_of(own_key, extent, cuts, -0.22, 0.18)
    return jnp.clip(array, -most, most).astype(kind)


def gaussian_with(own_key, extent, width, most, shards, heavy, kind=jnp.bfloat16):
    drawn = width * jax.random.normal(own_key, extent, jnp.float32)
    if shards:
        drawn = drawn * steps_of(own_key, extent, shards, -0.22, 0.18)
    return jnp.clip(raised(drawn, jax.random.fold_in(own_key, 3), *heavy), -most, most).astype(kind)


def setup_inputs(seed: int = 0) -> dict:
    arg_keys = jax.random.split(jax.random.key(seed), 22)
    return {
        "decoder_in": scatter_about(arg_keys[0], (TOKENS, D), 1.0, 6.0, ((0, 32),)),
        "encoder_out": scatter_about(arg_keys[1], (TOKENS, D), 1.0, 6.0, ((0, 32),)),
        "decoder_segments": draw_decoder_segments(jax.random.fold_in(arg_keys[21], 71), 0),
        "encoder_segments": draw_encoder_segments(jax.random.fold_in(arg_keys[21], 71), 0),
        "rel_buckets": draw_rel_buckets(jax.random.fold_in(arg_keys[21], 71), 0),
        "self_gain": jnp.clip(1.0 + 0.1 * jax.random.normal(arg_keys[5], (D,), jnp.float32), 0.5, 1.5),
        "self_query": scatter_about(arg_keys[6], (D, H * DH), (4 * D) ** -0.5, 0.109375, ((1, 2),)),
        "self_key": scatter_about(arg_keys[7], (D, H * DH), (4 * D) ** -0.5, 0.109375, ((1, 2),)),
        "self_value": scatter_about(arg_keys[8], (D, H * DH), D ** -0.5, 0.21875, ((1, 2),)),
        "self_output": scatter_about(arg_keys[9], (H * DH, D), (H * DH // 16) ** -0.5, 0.875, ((0, 2),)),
        "bias_table": scatter_about(arg_keys[10], (NB, H), 1.0, 4.0, ((1, 2),), jnp.float32),
        "cross_gain": jnp.clip(1.0 + 0.1 * jax.random.normal(arg_keys[11], (D,), jnp.float32), 0.5, 1.5),
        "cross_query": scatter_about(arg_keys[12], (D, H * DH), (4 * D) ** -0.5, 0.109375, ((1, 2),)),
        "cross_key": scatter_about(arg_keys[13], (D, H * DH), (4 * D) ** -0.5, 0.109375, ((1, 2),)),
        "cross_value": scatter_about(arg_keys[14], (D, H * DH), D ** -0.5, 0.21875, ((1, 2),)),
        "cross_output": scatter_about(arg_keys[15], (H * DH, D), (H * DH // 16) ** -0.5, 0.875, ((0, 2),)),
        "ffn_gain": jnp.clip(1.0 + 0.1 * jax.random.normal(arg_keys[16], (D,), jnp.float32), 0.5, 1.5),
        "ffn_gate": scatter_about(arg_keys[17], (D, FF), D ** -0.5, 0.21875),
        "ffn_up": scatter_about(arg_keys[18], (D, FF), D ** -0.5, 0.21875),
        "ffn_down": scatter_about(arg_keys[19], (FF, D), (FF // 4) ** -0.5, 0.25),
        "cotangent": gaussian_with(arg_keys[20], (TOKENS, D), 1.0, 6.0, ((0, 32),), (0, 1, 32, 2.75)),
    }


EPS = 1e-06
NEG = -1000000000.0
HIGH = lax.Precision.HIGHEST

@jax.custom_vjp
def low(v):
    return lax.optimization_barrier(v.astype(jnp.bfloat16)).astype(jnp.float32)

@jax.custom_vjp
def low_back(v):
    return v

def low_keep(v):
    return (low(v), None)

def low_pass(kept, grad):
    return (grad,)

def back_keep(v):
    return (v, None)

def back_low(kept, grad):
    return (low(grad),)
low.defvjp(low_keep, low_pass)
low_back.defvjp(back_keep, back_low)

def rms_scale(values, gain):
    return values * lax.rsqrt(lax.optimization_barrier(jnp.mean(values * values, axis=-1, keepdims=True)) + EPS) * gain

def project(left, weight):
    return jnp.einsum('bld,de->ble', left, weight, precision=HIGH)

def attend(query, keys, values, bias, masks):
    batch, length, _ = query.shape
    qh = query.reshape(batch, length, H, DH)
    kh = keys.reshape(batch, keys.shape[1], H, DH)
    vh = values.reshape(batch, values.shape[1], H, DH)
    scores = low_back(jnp.einsum('bqhd,bkhd->bhqk', qh, kh, precision=HIGH)) + bias
    scores = jnp.where(masks[:, None], scores, NEG)
    probs = low(jax.nn.softmax(scores, axis=-1))
    mixed = jnp.einsum('bhqk,bkhd->bqhd', probs, vh, precision=HIGH)
    return mixed.reshape(batch, length, H * DH)

def forward(weights, decoder, encoder, dseg, eseg, buckets, causal):
    gain_one, wq, wk, wv, wo, table, gain_two, cq, ck, cv, co, gain_three, wgate, wup, wdown = weights
    h_one = low(rms_scale(decoder, gain_one))
    query = low(low_back(project(h_one, wq)))
    keys = low(low_back(project(h_one, wk)))
    values = low(low_back(project(h_one, wv)))
    bias = jnp.transpose(table[buckets], (2, 0, 1))[None]
    mask_one = causal[None] & (dseg[:, :, None] == dseg[:, None, :])
    mixed = low(low_back(attend(query, keys, values, bias, mask_one)))
    x_two = decoder + low_back(project(mixed, wo))
    h_two = low(rms_scale(x_two, gain_two))
    query2 = low(low_back(project(h_two, cq)))
    keys2 = low(low_back(project(encoder, ck)))
    values2 = low(low_back(project(encoder, cv)))
    mask_two = dseg[:, :, None] == eseg[:, None, :]
    mixed2 = low(low_back(attend(query2, keys2, values2, 0.0, mask_two)))
    x_three = x_two + low_back(project(mixed2, co))
    h_three = low(rms_scale(x_three, gain_three))
    gate = low_back(project(h_three, wgate))
    upper = low_back(project(h_three, wup))
    hidden = low(jax.nn.gelu(gate, approximate=True) * upper)
    return x_three + low_back(project(hidden, wdown))

def reference(decoder_in, encoder_out, decoder_segments, encoder_segments, rel_buckets, self_gain, self_query, self_key, self_value, self_output, bias_table, cross_gain, cross_query, cross_key, cross_value, cross_output, ffn_gain, ffn_gate, ffn_up, ffn_down, cotangent):
    weights = tuple((w.astype(jnp.float32) for w in (self_gain, self_query, self_key, self_value, self_output, bias_table, cross_gain, cross_query, cross_key, cross_value, cross_output, ffn_gain, ffn_gate, ffn_up, ffn_down)))
    places = jnp.arange(LEN, dtype=jnp.int32)
    offset = places[:, None] - places[None, :]
    causal = offset >= 0
    buckets = rel_buckets[jnp.maximum(offset, 0).astype(jnp.int32)]
    group = 4
    while ROWS % group:
        group = group // 2
    nsteps = ROWS // group

    def split(a):
        return a.reshape((nsteps, group, LEN) + a.shape[1:])
    inputs = (split(decoder_in.astype(jnp.float32)), split(encoder_out.astype(jnp.float32)), decoder_segments.reshape(nsteps, group, LEN), encoder_segments.reshape(nsteps, group, LEN), split(cotangent.astype(jnp.float32)))

    def one_step(carry, xs):
        decoder, encoder, dseg, eseg, cot = xs

        def forward_fn(wts, dec_val, enc_val):
            return forward(wts, dec_val, enc_val, dseg, eseg, buckets, causal)
        result, pull = jax.vjp(forward_fn, weights, decoder, encoder)
        grads, grad_dec, grad_enc = pull(cot)
        carry = jax.tree.map(jnp.add, carry, grads)
        return (carry, (result, grad_dec, grad_enc))
    zeros = jax.tree.map(jnp.zeros_like, weights)
    grads, (result, grad_dec, grad_enc) = lax.scan(one_step, zeros, inputs)
    layer_out = result.reshape(TOKENS, D).astype(jnp.bfloat16)
    grad_decoder = grad_dec.reshape(TOKENS, D)
    grad_encoder = grad_enc.reshape(TOKENS, D)
    return (layer_out, grad_decoder, grad_encoder, grads[0], grads[1], grads[2], grads[3], grads[4], grads[5], grads[6], grads[7], grads[8], grads[9], grads[10], grads[11], grads[12], grads[13], grads[14])
```

```python
import functools

import jax
import jax.numpy as jnp
from jax import lax
from jax.experimental import pallas as pl
from jax.experimental.pallas import tpu as pltpu
from jax.sharding import PartitionSpec as P

EPS = 1e-06
NEG = -1000000000.0
HIGH = lax.Precision.HIGHEST
F32 = jnp.float32
BF16 = jnp.bfloat16
LANES = 128
BLOCK = 128


def dot(left, right):
    return jnp.dot(left, right, preferred_element_type=F32)


def dot_nt(left, right):
    return lax.dot_general(left, right, (((1,), (1,)), ((), ())), preferred_element_type=F32)


def dot_tn(left, right):
    return lax.dot_general(left, right, (((0,), (0,)), ((), ())), preferred_element_type=F32)


def vmem(count):
    return [pl.BlockSpec(memory_space=pltpu.VMEM)] * count


def kernel_call(body, inputs, outs, scratch=(), scalars=0, flops=0):
    shapes = [jax.ShapeDtypeStruct(s, d) for s, d in outs]
    nbytes = sum(a.size * a.dtype.itemsize for a in inputs)
    nbytes += sum(s.size * s.dtype.itemsize for s in shapes)
    return pl.pallas_call(
        body,
        out_shape=shapes,
        in_specs=[pl.BlockSpec(memory_space=pltpu.SMEM)] * scalars + vmem(len(inputs) - scalars),
        out_specs=vmem(len(shapes)),
        scratch_shapes=list(scratch),
        cost_estimate=pl.CostEstimate(flops=flops, bytes_accessed=nbytes, transcendentals=0),
        compiler_params=pltpu.CompilerParams(vmem_limit_bytes=56 * 1024 * 1024),
    )(*inputs)


def head_masks(head_dim):
    lane = lax.broadcasted_iota(jnp.int32, (1, LANES), 1)
    first = (lane < head_dim).astype(F32)
    return (first.astype(BF16), (1.0 - first).astype(BF16))


def normed(values, gain):
    return values * lax.rsqrt(jnp.mean(values * values, axis=-1, keepdims=True) + EPS) * gain


def strip_kernel(line_ref, strip_ref):
    heads, rows, width = strip_ref.shape
    span = line_ref.shape[1]
    for h in range(heads):
        wide = jnp.broadcast_to(line_ref[h : h + 1, :], (rows, span))
        strip_ref[h] = pltpu.roll(wide, 0, 1, stride=1, stride_axis=0)[:, :width]


def self_forward_kernel(
    place_ref, own_ref, other_ref, gain_ref, wq_ref, wk_ref, wv_ref, segc_ref, segr_ref, strip_ref,
    out_own_ref, out_other_ref, h1_ref, q_ref, k_ref, v_ref, p_ref, mixed_ref,
):
    half = own_ref.shape[0]
    length = half * 2
    place = place_ref[0]
    heads = p_ref.shape[0]
    head_dim = q_ref.shape[1] // heads
    own_rows = pl.ds(pl.multiple_of(place * half, half), half)
    other_rows = pl.ds(pl.multiple_of((1 - place) * half, half), half)
    for ref, rows in ((own_ref, own_rows), (other_ref, other_rows)):
        h1_ref[rows, :] = normed(ref[...].astype(F32), gain_ref[...]).astype(BF16)
    h1 = h1_ref[...]
    q_ref[...] = dot(h1, wq_ref[...]).astype(BF16)
    k_ref[...] = dot(h1, wk_ref[...]).astype(BF16)
    v_ref[...] = dot(h1, wv_ref[...]).astype(BF16)
    masks = head_masks(head_dim)

    def pair(hp, carry):
        lanes = pl.ds(pl.multiple_of(hp * LANES, LANES), LANES)
        for block in range(length // BLOCK):
            top = block * BLOCK
            seen = top + BLOCK
            shift = length - seen
            row = lax.broadcasted_iota(jnp.int32, (BLOCK, seen), 0) + top
            col = lax.broadcasted_iota(jnp.int32, (BLOCK, seen), 1)
            allowed = (col <= row) & (segc_ref[top:seen, :] == segr_ref[:, :seen])
            queries = q_ref[top:seen, lanes]
            keys = k_ref[:seen, lanes]
            values = v_ref[:seen, lanes]
            total = None
            for w in range(2):
                h = hp * 2 + w
                scores = dot_nt(queries * masks[w], keys) + strip_ref[h, :, shift:]
                scores = jnp.where(allowed, scores, NEG)
                expo = jnp.exp(scores - jnp.max(scores, axis=-1, keepdims=True))
                probs = (expo * (1.0 / jnp.sum(expo, axis=-1, keepdims=True))).astype(BF16)
                p_ref[h, top:seen, :seen] = probs
                part = dot(probs, values * masks[w])
                total = part if total is None else total + part
            mixed_ref[top:seen, lanes] = total.astype(BF16)
        return carry

    lax.fori_loop(0, heads // 2, pair, 0)
    out_own_ref[...] = mixed_ref[own_rows, :]
    out_other_ref[...] = mixed_ref[other_rows, :]


def diagonal_sums(strip):
    rows, span = strip.shape
    total = strip[:8]
    for top in range(8, rows, 8):
        total = total + pltpu.roll(strip[top : top + 8], span - top, 1)
    row = lax.broadcasted_iota(jnp.int32, total.shape, 0)
    for step in (1, 2, 4):
        total = jnp.where((row & step) != 0, pltpu.roll(total, span - step, 1), total)
    return jnp.sum(total, axis=0, keepdims=True)


def self_backward_kernel(
    place_ref, own_ref, other_ref, q_ref, k_ref, v_ref, p_ref,
    dq_ref, dk_ref, dv_ref, line_ref, do_ref, dka_ref, dva_ref, strip_ref,
):
    half = own_ref.shape[0]
    length = half * 2
    place = place_ref[0]
    heads = p_ref.shape[0]
    head_dim = q_ref.shape[1] // heads
    span = line_ref.shape[2]
    do_ref[pl.ds(pl.multiple_of(place * half, half), half), :] = own_ref[...]
    do_ref[pl.ds(pl.multiple_of((1 - place) * half, half), half), :] = other_ref[...]
    masks = head_masks(head_dim)

    def pair(hp, carry):
        lanes = pl.ds(pl.multiple_of(hp * LANES, LANES), LANES)
        dka_ref[...] = jnp.zeros_like(dka_ref)
        dva_ref[...] = jnp.zeros_like(dva_ref)
        strip_ref[...] = jnp.zeros_like(strip_ref)
        for block in range(length // BLOCK):
            top = block * BLOCK
            seen = top + BLOCK
            shift = length - seen
            queries = q_ref[top:seen, lanes]
            grads = do_ref[top:seen, lanes]
            keys = k_ref[:seen, lanes]
            values = v_ref[:seen, lanes]
            total = None
            for w in range(2):
                h = hp * 2 + w
                probs_low = p_ref[h, top:seen, :seen]
                probs = probs_low.astype(F32)
                dprob = dot_nt(grads * masks[w], values)
                delta = jnp.sum(dprob * probs, axis=-1, keepdims=True)
                dscore = probs * (dprob - delta)
                strip_ref[w, :, shift:length] += dscore
                dlow = dscore.astype(BF16)
                part = dot(dlow, keys * masks[w])
                total = part if total is None else total + part
                dka_ref[:seen, :] += dot_tn(dlow, queries * masks[w])
                dva_ref[:seen, :] += dot_tn(probs_low, grads * masks[w])
            dq_ref[top:seen, lanes] = total.astype(BF16)
        dk_ref[:, lanes] = dka_ref[...].astype(BF16)
        dv_ref[:, lanes] = dva_ref[...].astype(BF16)
        for w in range(2):
            line_ref[hp * 2 + w] = diagonal_sums(strip_ref[w])
        return carry

    lax.fori_loop(0, heads // 2, pair, 0)


def cross_forward_kernel(q_ref, k_ref, v_ref, segc_ref, segr_ref, out_ref, p_ref):
    heads = p_ref.shape[0]
    rows = q_ref.shape[0]
    masks = head_masks(q_ref.shape[1] // heads)

    def pair(hp, carry):
        lanes = pl.ds(pl.multiple_of(hp * LANES, LANES), LANES)
        keys = k_ref[:, lanes]
        values = v_ref[:, lanes]
        for block in range(rows // BLOCK):
            top = block * BLOCK
            allowed = segc_ref[top : top + BLOCK, :] == segr_ref[...]
            queries = q_ref[top : top + BLOCK, lanes]
            total = None
            for w in range(2):
                h = hp * 2 + w
                scores = jnp.where(allowed, dot_nt(queries * masks[w], keys), NEG)
                expo = jnp.exp(scores - jnp.max(scores, axis=-1, keepdims=True))
                probs = (expo * (1.0 / jnp.sum(expo, axis=-1, keepdims=True))).astype(BF16)
                p_ref[h, top : top + BLOCK, :] = probs
                part = dot(probs, values * masks[w])
                total = part if total is None else total + part
            out_ref[top : top + BLOCK, lanes] = total.astype(BF16)
        return carry

    lax.fori_loop(0, heads // 2, pair, 0)


def cross_backward_kernel(
    do_ref, q_ref, k_ref, v_ref, p_ref, dq_ref, dk_ref, dv_ref, dka_ref, dva_ref
):
    heads = p_ref.shape[0]
    rows = q_ref.shape[0]
    masks = head_masks(q_ref.shape[1] // heads)

    def pair(hp, carry):
        lanes = pl.ds(pl.multiple_of(hp * LANES, LANES), LANES)
        keys = k_ref[:, lanes]
        values = v_ref[:, lanes]
        dka_ref[...] = jnp.zeros_like(dka_ref)
        dva_ref[...] = jnp.zeros_like(dva_ref)
        for block in range(rows // BLOCK):
            top = block * BLOCK
            queries = q_ref[top : top + BLOCK, lanes]
            grads = do_ref[top : top + BLOCK, lanes]
            total = None
            for w in range(2):
                h = hp * 2 + w
                probs_low = p_ref[h, top : top + BLOCK, :]
                probs = probs_low.astype(F32)
                dprob = dot_nt(grads * masks[w], values)
                delta = jnp.sum(dprob * probs, axis=-1, keepdims=True)
                dlow = (probs * (dprob - delta)).astype(BF16)
                part = dot(dlow, keys * masks[w])
                total = part if total is None else total + part
                dka_ref[...] += dot_tn(dlow, queries * masks[w])
                dva_ref[...] += dot_tn(probs_low, grads * masks[w])
            dq_ref[top : top + BLOCK, lanes] = total.astype(BF16)
        dk_ref[:, lanes] = dka_ref[...].astype(BF16)
        dv_ref[:, lanes] = dva_ref[...].astype(BF16)
        return carry

    lax.fori_loop(0, heads // 2, pair, 0)


def swap_seq(value):
    return lax.ppermute(value, "seq", [(0, 1), (1, 0)])


def swap_dp(value, bit):
    size = lax.axis_size("dp")
    return lax.ppermute(value, "dp", [(i, i ^ (1 << bit)) for i in range(size)])


def picked(value, index, axis):
    return lax.dynamic_index_in_dim(value, index, axis, keepdims=False)


def fold(value, bits, order, place):
    left = list(bits)
    for bit in order:
        axis = left.index(bit)
        mine = (place >> bit) & 1
        value = picked(value, mine, axis) + swap_dp(picked(value, 1 - mine, axis), bit)
        left.remove(bit)
    return value


def local(
    decoder_in,
    encoder_out,
    decoder_segments,
    encoder_segments,
    rel_buckets,
    self_gain,
    self_query,
    self_key,
    self_value,
    self_output,
    bias_table,
    cross_gain,
    cross_query,
    cross_key,
    cross_value,
    cross_output,
    ffn_gain,
    ffn_gate,
    ffn_up,
    ffn_down,
    cotangent,
):
    dp_size = lax.axis_size("dp")
    seq_size = lax.axis_size("seq")
    place = lax.axis_index("seq")
    dp_place = lax.axis_index("dp")
    nbits = dp_size.bit_length() - 1
    bits = tuple(range(nbits - 1, -1, -1))
    order = tuple(range(nbits))
    core = dp_place & 1
    half, width = decoder_in.shape
    length = decoder_segments.shape[1]
    heads_here = bias_table.shape[1]
    buckets_all = bias_table.shape[0]
    cols = self_query.shape[1]
    hidden_dim = ffn_gate.shape[1]
    places = jnp.reshape(place, (1,)).astype(jnp.int32)

    decoder_far = swap_seq(decoder_in)
    encoder_far = swap_seq(encoder_out)

    def far_weight(weight):
        rows = weight.shape[0] // 2
        piece = swap_seq(lax.dynamic_slice_in_dim(weight, core * rows, rows, 0))
        mate = swap_dp(piece, 0)
        whole = jnp.concatenate([piece, mate], axis=0)
        turned = jnp.concatenate([mate, piece], axis=0)
        return jnp.where(core == 0, whole, turned)

    out_far, cq_far, ck_far, cv_far, co_far = [
        far_weight(w) for w in (self_output, cross_query, cross_key, cross_value, cross_output)
    ]

    span = length + LANES
    near = length - BLOCK
    line_buckets = jnp.concatenate(
        [
            rel_buckets[: near + 1][::-1],
            jnp.full((span - length,), -1, jnp.int32),
            rel_buckets[near + 1 :][::-1],
        ]
    )
    onehot = (
        line_buckets[:, None] == jnp.arange(buckets_all, dtype=jnp.int32)[None, :]
    ).astype(F32)
    line = jnp.einsum("bh,tb->ht", bias_table, onehot, precision=HIGH)
    (strip,) = kernel_call(strip_kernel, (line,), [((heads_here, BLOCK, length), F32)])

    segc = decoder_segments.reshape(length, 1)
    mixed_own, mixed_other, h1, q1, k1, v1, p1 = kernel_call(
        self_forward_kernel,
        (
            places, decoder_in, decoder_far, self_gain.reshape(1, width),
            self_query, self_key, self_value, segc, decoder_segments, strip,
        ),
        [
            ((half, cols), BF16), ((half, cols), BF16), ((length, width), BF16),
            ((length, cols), BF16), ((length, cols), BF16), ((length, cols), BF16),
            ((heads_here, length, length), BF16),
        ],
        scratch=(pltpu.VMEM((length, cols), BF16),),
        scalars=1,
        flops=2 * length * width * cols * 3 + 4 * length * length * cols,
    )
    mixed_far = swap_seq(mixed_other)

    encoder_full = jnp.concatenate([encoder_out, encoder_far], axis=0)
    ck_all = jnp.concatenate([cross_key, ck_far], axis=1)
    cv_all = jnp.concatenate([cross_value, cv_far], axis=1)
    cq_all = jnp.concatenate([cross_query, cq_far], axis=1)
    co_all = jnp.concatenate([cross_output, co_far], axis=0)
    so_all = jnp.concatenate([self_output, out_far], axis=0)
    k2 = dot(encoder_full, ck_all).astype(BF16)
    v2 = dot(encoder_full, cv_all).astype(BF16)

    decoder = decoder_in.astype(F32)
    mixed_one = jnp.concatenate([mixed_own, mixed_far], axis=1)
    x_two = decoder + dot(mixed_one, so_all)
    normed_two, back_two = jax.vjp(normed, x_two, cross_gain)
    h2 = normed_two.astype(BF16)
    q2 = dot(h2, cq_all).astype(BF16)
    dseg = lax.dynamic_slice_in_dim(segc, place * half, half, 0)
    eseg = jnp.roll(encoder_segments, -place * half, axis=1)
    heads_all = heads_here * seq_size
    mixed_two, p2 = kernel_call(
        cross_forward_kernel,
        (q2, k2, v2, dseg, eseg),
        [((half, width), BF16), ((heads_all, half, length), BF16)],
        flops=4 * half * length * width,
    )
    x_three = x_two + dot(mixed_two, co_all)
    normed_three, back_three = jax.vjp(normed, x_three, ffn_gain)
    h3 = normed_three.astype(BF16)
    gate = dot(h3, ffn_gate)
    upper = dot(h3, ffn_up)
    hidden, back_gated = jax.vjp(lambda a, b: jax.nn.gelu(a, approximate=True) * b, gate, upper)
    hidden = hidden.astype(BF16)
    layer_out = (x_three + dot(hidden, ffn_down)).astype(BF16)

    grad_hidden = dot_nt(cotangent, ffn_down)
    grad_gate, grad_upper = back_gated(grad_hidden)
    grad_gate = grad_gate.astype(BF16)
    grad_upper = grad_upper.astype(BF16)
    ffn_rows = hidden_dim // (dp_size * seq_size)

    def ffn_sum(left, right):
        value = dot_tn(left, right).astype(BF16)
        value = value.reshape((2,) * nbits + (seq_size, ffn_rows, width))
        axis = nbits
        mine = (dp_place & 1)
        value = picked(value, mine, nbits - 1) + swap_dp(picked(value, 1 - mine, nbits - 1), 0)
        value = picked(value, place, nbits - 1) + swap_seq(picked(value, 1 - place, nbits - 1))
        return fold(value, bits[:-1], order[1:], dp_place).astype(F32)

    ffn_sums = (
        ffn_sum(grad_gate, h3).T,
        ffn_sum(grad_upper, h3).T,
        ffn_sum(hidden, cotangent),
    )
    grad_h3 = dot_nt(grad_gate, ffn_gate) + dot_nt(grad_upper, ffn_up)
    grad_x_three, gain_three = back_three(grad_h3)
    grad_x_three = cotangent.astype(F32) + grad_x_three

    dc = grad_x_three.astype(BF16)
    do2 = dot_nt(dc, co_all).astype(BF16)
    dq2, dk2, dv2 = kernel_call(
        cross_backward_kernel,
        (do2, q2, k2, v2, p2),
        [((half, width), BF16), ((length, width), BF16), ((length, width), BF16)],
        scratch=(pltpu.VMEM((length, LANES), F32), pltpu.VMEM((length, LANES), F32)),
        flops=8 * half * length * width,
    )

    def whole_sum(left, right):
        value = dot_tn(left, right).astype(BF16)
        near_part = value[:, :cols].reshape((2,) * nbits + (width // dp_size, cols))
        far_part = value[:, cols:].reshape((2,) * nbits + (width // dp_size, cols))
        mine = dp_place & 1
        ax = nbits - 1
        near_part = picked(near_part, mine, ax) + swap_dp(picked(near_part, 1 - mine, ax), 0)
        far_part = picked(far_part, mine, ax) + swap_dp(picked(far_part, 1 - mine, ax), 0)
        value = near_part + swap_seq(far_part)
        return fold(value, bits[:-1], order[1:], dp_place).astype(F32)

    sum_co = whole_sum(dc, mixed_two).T
    sum_cq = whole_sum(h2, dq2)
    sum_ck = whole_sum(encoder_full, dk2)
    sum_cv = whole_sum(encoder_full, dv2)
    grad_h2 = dot_nt(dq2, cq_all)
    toward_encoder = dot_nt(dk2, ck_all) + dot_nt(dv2, cv_all)
    grad_encoder = toward_encoder[:half] + swap_seq(toward_encoder[half:].astype(BF16)).astype(F32)
    grad_x_two, gain_two = back_two(grad_h2)
    grad_x_two = grad_x_three + grad_x_two

    dy = grad_x_two.astype(BF16)
    do1 = dot_nt(dy, so_all).astype(BF16)
    do1_far = swap_seq(do1[:, cols:])
    sum_so = whole_sum(dy, mixed_one).T
    dq1, dk1, dv1, line_grads = kernel_call(
        self_backward_kernel,
        (places, do1[:, :cols], do1_far, q1, k1, v1, p1),
        [
            ((length, cols), BF16), ((length, cols), BF16), ((length, cols), BF16),
            ((heads_here, 1, span), F32),
        ],
        scratch=(
            pltpu.VMEM((length, cols), BF16), pltpu.VMEM((length, LANES), F32),
            pltpu.VMEM((length, LANES), F32), pltpu.VMEM((2, BLOCK, span), F32),
        ),
        scalars=1,
        flops=8 * length * length * cols,
    )
    toward_h1 = dot_nt(dq1, self_query) + dot_nt(dk1, self_key) + dot_nt(dv1, self_value)
    h1_other = lax.dynamic_slice_in_dim(toward_h1, (1 - place) * half, half, 0).astype(BF16)
    h1_own = lax.dynamic_slice_in_dim(toward_h1, place * half, half, 0)
    grad_h1 = h1_own + swap_seq(h1_other).astype(F32)

    def head_sum(right):
        value = dot_tn(h1, right).astype(BF16).reshape((2,) * nbits + (width // dp_size, cols))
        return fold(value, bits, order, dp_place).astype(F32)

    sum_q, sum_k, sum_v = head_sum(dq1), head_sum(dk1), head_sum(dv1)
    _, back_one = jax.vjp(normed, decoder, self_gain)
    grad_decoder, gain_one = back_one(grad_h1)
    grad_decoder = grad_x_two + grad_decoder

    table_local = jnp.einsum("ht,tb->bh", line_grads[:, 0, :], onehot, precision=HIGH)
    table_full = lax.dynamic_update_slice(
        jnp.zeros((buckets_all, heads_all), F32), table_local, (0, place * heads_here)
    )
    small = jnp.concatenate([gain_one, gain_two, gain_three, table_full.reshape(-1)])
    small = small.reshape(-1, LANES)
    small = small + swap_seq(small)
    for bit in order:
        small = small + swap_dp(small, bit)
    small = small.reshape(-1)
    gain_one, gain_two, gain_three = small[:width], small[width : 2 * width], small[2 * width : 3 * width]
    table_sum = small[3 * width :].reshape(buckets_all, heads_all)
    return (
        layer_out, grad_decoder, grad_encoder, gain_one, sum_q, sum_k, sum_v, sum_so, table_sum,
        gain_two, sum_cq, sum_ck, sum_cv, sum_co, gain_three, *ffn_sums,
    )


def solution(mesh):
    tokens, both = P(("dp", "seq"), None), P("dp", "seq")
    col, row = P(None, "seq"), P("seq", None)
    return jax.shard_map(
        local,
        mesh=mesh,
        in_specs=(
            tokens, tokens, P("dp", None), P("dp", None), P(), P(), col, col, col, row, col,
            P(), col, col, col, row, P(), P(), P(), P(), tokens,
        ),
        out_specs=(
            tokens, tokens, tokens, P(), both, both, both, P("seq", "dp"), P(), P(), both, both,
            both, P("seq", "dp"), P(), P(None, ("dp", "seq")), P(None, ("dp", "seq")), tokens,
        ),
        check_vma=False,
    )
```

```python
import functools

import jax
import jax.numpy as jnp
from jax import lax
from jax.experimental import pallas as pl
from jax.experimental.pallas import tpu as pltpu
from jax.sharding import PartitionSpec as P

EPS = 1e-06
NEG = -1000000000.0
HIGH = lax.Precision.HIGHEST
F32 = jnp.float32
BF16 = jnp.bfloat16
LANES = 128
BLOCK = 128


def dot(left, right):
    return jnp.dot(left, right, preferred_element_type=F32)


def dot_nt(left, right):
    return lax.dot_general(left, right, (((1,), (1,)), ((), ())), preferred_element_type=F32)


def dot_tn(left, right):
    return lax.dot_general(left, right, (((0,), (0,)), ((), ())), preferred_element_type=F32)


class Incoming:
    def __init__(self, ref):
        self.ref = ref

    def get(self):
        return self.ref


class Outgoing:
    def __init__(self, ref):
        self.ref = ref


def kernel_call(body, inputs, outs, scratch=(), scalars=0, flops=0, tokens=(), mib=12):
    shapes = [jax.ShapeDtypeStruct(s, d) for s, d in outs]
    nbytes = sum(a.size * a.dtype.itemsize for a in inputs)
    nbytes += sum(s.size * s.dtype.itemsize for s in shapes)
    reads, skipped, writes = len(inputs), len(tokens), len(outs)

    def run(*refs):
        ins, rest = refs[:reads], refs[reads + skipped :]
        body(
            *ins[:scalars],
            *[Incoming(ref) for ref in ins[scalars:]],
            *[Outgoing(ref) for ref in rest[:writes]],
            *rest[writes:],
        )

    in_vmem = pl.BlockSpec(memory_space=pltpu.VMEM)
    return pl.pallas_call(
        run,
        out_shape=shapes,
        in_specs=[pl.BlockSpec(memory_space=pltpu.SMEM)] * scalars
        + [in_vmem] * (reads - scalars)
        + [pl.BlockSpec(memory_space=pl.ANY)] * skipped,
        out_specs=[in_vmem] * writes,
        scratch_shapes=list(scratch),
        cost_estimate=pl.CostEstimate(flops=flops, bytes_accessed=nbytes, transcendentals=0),
        compiler_params=pltpu.CompilerParams(vmem_limit_bytes=mib * 1024 * 1024),
    )(*inputs, *tokens)


def head_masks(head_dim):
    lane = lax.broadcasted_iota(jnp.int32, (1, LANES), 1)
    first = (lane < head_dim).astype(F32)
    return (first.astype(BF16), (1.0 - first).astype(BF16))


def normed(values, gain):
    return values * lax.rsqrt(jnp.mean(values * values, axis=-1, keepdims=True) + EPS) * gain


def inverse_rms(values):
    return lax.rsqrt(jnp.mean(values * values, axis=-1, keepdims=True) + EPS)


def normed_back(values, gain, grads):
    scale = inverse_rms(values)
    scaled = grads * gain
    mean = jnp.mean(values * scaled, axis=-1, keepdims=True)
    toward = scale * scaled - values * (scale * scale * scale * mean)
    return toward, jnp.sum(grads * values * scale, axis=0, keepdims=True)


def strip_kernel(line_in, strip_out):
    line, strip = line_in.get(), strip_out.ref
    heads, rows, width = strip.shape
    span = line.shape[1]
    for h in range(heads):
        wide = jnp.broadcast_to(line[h : h + 1, :], (rows, span))
        strip[h] = pltpu.roll(wide, 0, 1, stride=1, stride_axis=0)[:, :width]


def softmax_low(scores):
    expo = jnp.exp(scores - jnp.max(scores, axis=-1, keepdims=True))
    return (expo * (1.0 / jnp.sum(expo, axis=-1, keepdims=True))).astype(BF16)


def self_forward_kernel(
    place_ref, own_in, gain_in, wq_in, other_in, wk_in, wv_in, segc_in, segr_in, strip_in,
    out_own, out_other, h1_out, q_out, k_out, v_out, p_out, mixed_ref,
):
    half = own_in.ref.shape[0]
    length = half * 2
    place = place_ref[0]
    q_ref, k_ref, v_ref, p_ref, h1_ref = q_out.ref, k_out.ref, v_out.ref, p_out.ref, h1_out.ref
    heads = p_ref.shape[0]
    own_rows = pl.ds(pl.multiple_of(place * half, half), half)
    other_rows = pl.ds(pl.multiple_of((1 - place) * half, half), half)
    gain = gain_in.get()[...]
    for array, rows in ((own_in, own_rows), (other_in, other_rows)):
        h1_ref[rows, :] = normed(array.get()[...].astype(F32), gain).astype(BF16)
    h1 = h1_ref[...]
    for weight, out in ((wq_in, q_out), (wk_in, k_out), (wv_in, v_out)):
        out.ref[...] = dot(h1, weight.get()[...]).astype(BF16)
    masks = head_masks(q_ref.shape[1] // heads)
    segc_ref, segr_ref, strip_ref = segc_in.get(), segr_in.get(), strip_in.get()

    def pair(hp, carry):
        lanes = pl.ds(pl.multiple_of(hp * LANES, LANES), LANES)
        for block in range(length // BLOCK):
            top = block * BLOCK
            seen = top + BLOCK
            shift = length - seen
            row = lax.broadcasted_iota(jnp.int32, (BLOCK, seen), 0) + top
            col = lax.broadcasted_iota(jnp.int32, (BLOCK, seen), 1)
            allowed = (col <= row) & (segc_ref[top:seen, :] == segr_ref[:, :seen])
            queries = q_ref[top:seen, lanes]
            keys = k_ref[:seen, lanes]
            values = v_ref[:seen, lanes]
            total = None
            for w in range(2):
                h = hp * 2 + w
                scores = dot_nt(queries * masks[w], keys) + strip_ref[h, :, shift:]
                probs = softmax_low(jnp.where(allowed, scores, NEG))
                p_ref[h, top:seen, :seen] = probs
                part = dot(probs, values * masks[w])
                total = part if total is None else total + part
            mixed_ref[top:seen, lanes] = total.astype(BF16)
        return carry

    lax.fori_loop(0, heads // 2, pair, 0)
    out_other.ref[...] = mixed_ref[other_rows, :]
    out_own.ref[...] = mixed_ref[own_rows, :]


def diagonal_sums(strip):
    rows, span = strip.shape
    total = strip[:8]
    for top in range(8, rows, 8):
        total = total + pltpu.roll(strip[top : top + 8], span - top, 1)
    row = lax.broadcasted_iota(jnp.int32, total.shape, 0)
    for step in (1, 2, 4):
        total = jnp.where((row & step) != 0, pltpu.roll(total, span - step, 1), total)
    return jnp.sum(total, axis=0, keepdims=True)


def self_backward_kernel(
    place_ref, q_in, k_in, v_in, own_in, other_in, p_in, wq_in, wk_in, wv_in, x_own_in, x_other_in,
    grads_out, line_out, h1_own_out, h1_other_out, gain_out,
    do_ref, dka_ref, dva_ref, strip_ref,
):
    p_ref = p_in.get()
    half = own_in.ref.shape[0]
    length = half * 2
    place = place_ref[0]
    heads = p_ref.shape[0]
    own_rows = pl.ds(pl.multiple_of(place * half, half), half)
    other_rows = pl.ds(pl.multiple_of((1 - place) * half, half), half)
    q_ref, k_ref, v_ref = q_in.get(), k_in.get(), v_in.get()
    dq_ref, dk_ref, dv_ref = (grads_out.ref.at[at] for at in range(3))
    do_ref[own_rows, :] = own_in.get()[...]
    do_ref[other_rows, :] = other_in.get()[...]
    masks = head_masks(q_ref.shape[1] // heads)
    line_ref = line_out.ref

    def pair(hp, carry):
        lanes = pl.ds(pl.multiple_of(hp * LANES, LANES), LANES)
        dka_ref[...] = jnp.zeros_like(dka_ref)
        dva_ref[...] = jnp.zeros_like(dva_ref)
        strip_ref[...] = jnp.zeros_like(strip_ref)
        for block in range(length // BLOCK):
            top = block * BLOCK
            seen = top + BLOCK
            shift = length - seen
            queries = q_ref[top:seen, lanes]
            grads = do_ref[top:seen, lanes]
            keys = k_ref[:seen, lanes]
            values = v_ref[:seen, lanes]
            total = None
            for w in range(2):
                probs_low = p_ref[hp * 2 + w, top:seen, :seen]
                probs = probs_low.astype(F32)
                dprob = dot_nt(grads * masks[w], values)
                delta = jnp.sum(dprob * probs, axis=-1, keepdims=True)
                dscore = probs * (dprob - delta)
                strip_ref[w, :, shift:length] += dscore
                dlow = dscore.astype(BF16)
                part = dot(dlow, keys * masks[w])
                total = part if total is None else total + part
                dka_ref[:seen, :] += dot_tn(dlow, queries * masks[w])
                dva_ref[:seen, :] += dot_tn(probs_low, grads * masks[w])
            dq_ref[top:seen, lanes] = total.astype(BF16)
        dk_ref[:, lanes] = dka_ref[...].astype(BF16)
        dv_ref[:, lanes] = dva_ref[...].astype(BF16)
        for w in range(2):
            line_ref[hp * 2 + w] = diagonal_sums(strip_ref[w])
        return carry

    lax.fori_loop(0, heads // 2, pair, 0)
    weights = wq_in.get(), wk_in.get(), wv_in.get()
    gain = jnp.zeros(gain_out.ref.shape, F32)
    for out, rows, x_in in ((h1_other_out, other_rows, x_other_in), (h1_own_out, own_rows, x_own_in)):
        toward = dot_nt(dq_ref[rows, :], weights[0][...])
        toward = toward + dot_nt(dk_ref[rows, :], weights[1][...]) + dot_nt(dv_ref[rows, :], weights[2][...])
        out.ref[...] = toward.astype(out.ref.dtype)
        values = x_in.get()[...].astype(F32)
        gain = gain + jnp.sum(toward * values * inverse_rms(values), axis=0, keepdims=True)
    gain_out.ref[...] = gain


def unpack_kernel(place_ref, *refs):
    wide, tall = refs[:4], refs[4:8]
    own_in, far_in, ck_in, cv_in = refs[8:12]
    so_out, co_out, cq_out, ck_out, cv_out, k_out, v_out, enc_out = refs[12:]
    half, cols = own_in.ref.shape[0], ck_in.ref.shape[1]
    for relative in range(4):
        piece = wide[relative].get()
        rows = piece.shape[0] // 2
        to = pl.ds(pl.multiple_of((place_ref[0] ^ relative) * rows, rows), rows)
        so_out.ref[to, :] = piece[:rows, :]
        co_out.ref[to, :] = piece[rows:, :]
        piece = tall[relative].get()
        rows = piece.shape[0]
        to = pl.ds(pl.multiple_of((place_ref[1] ^ relative) * rows, rows), rows)
        for slot, out in enumerate((cq_out, ck_out, cv_out)):
            out.ref[to, :] = piece[:, slot * cols : (slot + 1) * cols]
    enc = enc_out.ref
    enc[:half, :] = own_in.get()[...]
    enc[half:, :] = far_in.get()[...]
    for near, far, out in ((ck_in.get(), ck_out.ref, k_out), (cv_in.get(), cv_out.ref, v_out)):
        out.ref[:, :cols] = dot(enc[...], near[...]).astype(BF16)
        out.ref[:, cols:] = dot(enc[...], far[...]).astype(BF16)


def middle_kernel(
    x_in, mixed_own_in, so_in, mixed_far_in, so_far_in, gain_in, cq_in, cq_far_in,
    k_in, v_in, segc_in, segr_in, co_in, co_far_in, next_gain_in,
    x_two_out, stack_out, q_out, p_out, x_three_out,
):
    half, cols = mixed_own_in.ref.shape
    q_ref, p_ref = q_out.ref, p_out.ref
    h2_ref, out_ref, h3_ref, mixed_ref = (stack_out.ref.at[at * half : (at + 1) * half] for at in range(4))
    mixed_ref[:, :cols] = mixed_own_in.get()[...]
    mixed_ref[:, cols:] = mixed_far_in.get()[...]
    x_two = x_in.get()[...].astype(F32) + dot(mixed_ref[:, :cols], so_in.get()[...])
    x_two = x_two + dot(mixed_ref[:, cols:], so_far_in.get()[...])
    x_two_out.ref[...] = x_two
    h2 = normed(x_two, gain_in.get()[...]).astype(BF16)
    h2_ref[...] = h2
    q_ref[:, :cols] = dot(h2, cq_in.get()[...]).astype(BF16)
    q_ref[:, cols:] = dot(h2, cq_far_in.get()[...]).astype(BF16)
    heads = p_ref.shape[0]
    masks = head_masks(q_ref.shape[1] // heads)
    k_ref, v_ref, segc_ref, segr_ref = k_in.get(), v_in.get(), segc_in.get(), segr_in.get()

    def pair(hp, carry):
        lanes = pl.ds(pl.multiple_of(hp * LANES, LANES), LANES)
        keys = k_ref[:, lanes]
        values = v_ref[:, lanes]
        for block in range(half // BLOCK):
            top = block * BLOCK
            allowed = segc_ref[top : top + BLOCK, :] == segr_ref[...]
            queries = q_ref[top : top + BLOCK, lanes]
            total = None
            for w in range(2):
                h = hp * 2 + w
                probs = softmax_low(jnp.where(allowed, dot_nt(queries * masks[w], keys), NEG))
                p_ref[h, top : top + BLOCK, :] = probs
                part = dot(probs, values * masks[w])
                total = part if total is None else total + part
            out_ref[top : top + BLOCK, lanes] = total.astype(BF16)
        return carry

    lax.fori_loop(0, heads // 2, pair, 0)
    x_three = x_two_out.ref[...] + dot(out_ref[:, :cols], co_in.get()[...])
    x_three = x_three + dot(out_ref[:, cols:], co_far_in.get()[...])
    x_three_out.ref[...] = x_three
    h3_ref[...] = normed(x_three, next_gain_in.get()[...]).astype(BF16)


def ffn_kernel(source_ref, x_ref, h_ref, cot_ref, *refs):
    del source_ref
    count = (len(refs) - 13) // 3
    gates, ups, downs = refs[:count], refs[count : 2 * count], refs[2 * count : 3 * count]
    (
        gain_ref, co_ref, co_far_ref, out_ref, keep_ref, send_ref, dx_ref, dc_ref, do_ref, dgain_ref,
        sum_ref, dh_ref, _,
    ) = refs[3 * count :]
    step, steps = pl.program_id(0), pl.num_programs(0)
    cols = co_ref.shape[0]

    @pl.when(step == 0)
    def _():
        sum_ref[...] = x_ref[...]
        dh_ref[...] = jnp.zeros_like(dh_ref)

    h = h_ref[...]
    gate_w = jnp.concatenate([ref[...] for ref in gates], axis=1)
    up_w = jnp.concatenate([ref[...] for ref in ups], axis=1)
    down_w = jnp.concatenate([ref[...] for ref in downs], axis=0)
    gate = dot(h, gate_w)
    upper = dot(h, up_w)
    dhidden = dot_nt(cot_ref[...], down_w)
    square = gate * gate
    inner = 0.7978845608028654 * gate * (1.0 + 0.044715 * square)
    bent = jnp.tanh(inner)
    factor = 0.5 * (1.0 + bent)
    gelu = gate * factor
    slope = factor + (0.5 * 0.7978845608028654) * gate * (1.0 - bent * bent) * (1.0 + 0.134145 * square)
    hidden = (gelu * upper).astype(BF16)
    dgate = (dhidden * upper * slope).astype(BF16)
    dup = (dhidden * gelu).astype(BF16)

    def put(ref):
        ref[0] = dgate
        ref[1] = dup
        ref[2] = hidden

    pl.when(step < steps // 2)(lambda: put(keep_ref))
    pl.when(step >= steps // 2)(lambda: put(send_ref))
    sum_ref[...] += dot(hidden, down_w)
    dh_ref[...] += dot_nt(dgate, gate_w) + dot_nt(dup, up_w)

    @pl.when(step == steps - 1)
    def _():
        out_ref[...] = sum_ref[...].astype(BF16)
        toward, dgain = normed_back(x_ref[...], gain_ref[...], dh_ref[...])
        dgain_ref[...] = dgain
        dx = cot_ref[...].astype(F32) + toward
        dx_ref[...] = dx
        dc = dx.astype(BF16)
        dc_ref[...] = dc
        do_ref[:, :cols] = dot_nt(dc, co_ref[...]).astype(BF16)
        do_ref[:, cols:] = dot_nt(dc, co_far_ref[...]).astype(BF16)


def ffn_call(source, x_three, stack, cot, gate_w, up_w, down_w, gain, co, co_far, steps=4):
    half, width = x_three.shape
    hidden = gate_w.shape[1]
    chunk = hidden // steps
    count = chunk // LANES

    def whole(array):
        return pl.BlockSpec(array.shape, lambda i, src: (0, 0))

    def col(at):
        return pl.BlockSpec((width, LANES), lambda i, src: (0, src[i * count + at]))

    def row(at):
        return pl.BlockSpec((LANES, width), lambda i, src: (src[i * count + at], 0))

    tokens = pl.BlockSpec((half, width), lambda i, src: (0, 0))
    third = pl.BlockSpec((half, width), lambda i, src: (2, 0))
    turn = steps // 2
    keep = pl.BlockSpec((3, half, chunk), lambda i, src: (0, 0, jnp.minimum(i, turn - 1)))
    send = pl.BlockSpec((3, half, chunk), lambda i, src: (0, 0, jnp.maximum(i - turn, 0)))
    shapes = [
        ((half, width), BF16), ((3, half, hidden // 2), BF16), ((3, half, hidden // 2), BF16),
        ((half, width), F32), ((half, width), BF16), ((half, width), BF16), ((1, width), F32),
    ]
    weights = [col(at) for at in range(count)] * 2 + [row(at) for at in range(count)]
    return pl.pallas_call(
        ffn_kernel,
        grid_spec=pltpu.PrefetchScalarGridSpec(
            num_scalar_prefetch=1,
            grid=(steps,),
            in_specs=[tokens, third, tokens] + weights + [whole(gain), whole(co), whole(co_far)],
            out_specs=[tokens, keep, send, tokens, tokens, tokens, whole(gain)],
            scratch_shapes=[pltpu.VMEM((half, width), F32), pltpu.VMEM((half, width), F32), pltpu.SMEM((1,), jnp.int32)],
        ),
        out_shape=[jax.ShapeDtypeStruct(s, d) for s, d in shapes],
        cost_estimate=pl.CostEstimate(
            flops=12 * half * width * hidden, bytes_accessed=6 * width * hidden, transcendentals=0
        ),
        compiler_params=pltpu.CompilerParams(vmem_limit_bytes=18 * 1024 * 1024),
    )(
        source, x_three, stack, cot, *[gate_w] * count, *[up_w] * count, *[down_w] * count, gain, co, co_far
    )


def cross_backward_kernel(
    do_in, q_in, k_in, v_in, p_in, cq_in, cq_far_in, x_two_in, gain_in, dx_in, so_in, so_far_in,
    stack_out, dx_two_out, do_own_out, do_other_out, dgain_out, dka_ref, dva_ref,
):
    p_ref = p_in.get()
    heads = p_ref.shape[0]
    rows, cols = q_in.ref.shape[0], cq_in.ref.shape[1]
    length = k_in.ref.shape[0]
    do_ref, v_ref, q_ref, k_ref = do_in.get(), v_in.get(), q_in.get(), k_in.get()
    masks = head_masks(q_ref.shape[1] // heads)
    dq_ref = stack_out.ref.at[:rows]
    dk_ref = stack_out.ref.at[rows : rows + length]
    dv_ref = stack_out.ref.at[rows + length : rows + 2 * length]
    dy_ref = stack_out.ref.at[rows + 2 * length :]

    def pair(hp, carry):
        lanes = pl.ds(pl.multiple_of(hp * LANES, LANES), LANES)
        keys = k_ref[:, lanes]
        values = v_ref[:, lanes]
        dka_ref[...] = jnp.zeros_like(dka_ref)
        dva_ref[...] = jnp.zeros_like(dva_ref)
        for block in range(rows // BLOCK):
            top = block * BLOCK
            queries = q_ref[top : top + BLOCK, lanes]
            grads = do_ref[top : top + BLOCK, lanes]
            total = None
            for w in range(2):
                probs_low = p_ref[hp * 2 + w, top : top + BLOCK, :]
                probs = probs_low.astype(F32)
                dprob = dot_nt(grads * masks[w], values)
                delta = jnp.sum(dprob * probs, axis=-1, keepdims=True)
                dlow = (probs * (dprob - delta)).astype(BF16)
                part = dot(dlow, keys * masks[w])
                total = part if total is None else total + part
                dka_ref[...] += dot_tn(dlow, queries * masks[w])
                dva_ref[...] += dot_tn(probs_low, grads * masks[w])
            dq_ref[top : top + BLOCK, lanes] = total.astype(BF16)
        dk_ref[:, lanes] = dka_ref[...].astype(BF16)
        dv_ref[:, lanes] = dva_ref[...].astype(BF16)
        return carry

    lax.fori_loop(0, heads // 2, pair, 0)
    dh2 = dot_nt(dq_ref[:, :cols], cq_in.get()[...]) + dot_nt(dq_ref[:, cols:], cq_far_in.get()[...])
    toward, dgain = normed_back(x_two_in.get()[...], gain_in.get()[...], dh2)
    dgain_out.ref[...] = dgain
    dx_two = dx_in.get()[...] + toward
    dy = dx_two.astype(BF16)
    dy_ref[...] = dy
    dx_two_out.ref[...] = dx_two
    do_other_out.ref[...] = dot_nt(dy, so_far_in.get()[...]).astype(BF16)
    do_own_out.ref[...] = dot_nt(dy, so_in.get()[...]).astype(BF16)


class Part:
    def __init__(self, rows, axes):
        self.rows, self.axes = rows, axes
        self.kept = self.arriving = None


def lay_out(parts):
    kept, sent, places = 0, {}, []
    for part in parts:
        rows, axis = part.rows // 2, part.axes[0]
        places.append((kept, axis, sent.get(axis, 0)))
        kept += rows
        sent[axis] = sent.get(axis, 0) + rows
    return kept, sent, places


def launched(parts, arrays, swap):
    kept, sent, places = lay_out(parts)
    arriving = {axis: swap(array, axis) for axis, array in zip(sent, arrays[1:])}
    moved = []
    for part, (at, axis, sent_at) in zip(parts, places):
        new = Part(part.rows // 2, part.axes[1:])
        new.kept, new.arriving = (arrays[0], at), (arriving[axis], sent_at)
        moved.append(new)
    return moved


def out_shapes(parts, lanes):
    kept, sent, _ = lay_out(parts)
    return [((kept, lanes), BF16)] + [((rows, lanes), BF16) for rows in sent.values()]


def writer(parts, outs):
    _, sent, places = lay_out(parts)
    refs = dict(zip(sent, (out.ref for out in outs[1:])))

    def put(at, index, value):
        eighth = parts[at].rows // 8
        kept_at, axis, sent_at = places[at]
        ref, base = (outs[0].ref, kept_at) if index < 4 else (refs[axis], sent_at)
        first = base + (index % 4) * eighth
        ref[first : first + eighth, :] = value

    return put


def position(axes, index):
    where = 0
    for axis in axes[:3]:
        where = where * 2 + index[axis]
    return where


def arrays_of(parts):
    arrays = []
    for part in parts:
        for array, _ in (part.kept, part.arriving):
            if not any(array is known for known in arrays):
                arrays.append(array)

    def find(pair):
        return next(at for at, known in enumerate(arrays) if known is pair[0]), pair[1]

    return arrays, [(find(part.kept), find(part.arriving)) for part in parts]


def stepped(parts, swap, tokens=()):
    arrays, spots = arrays_of(parts)
    lanes = arrays[0].shape[1]
    _, sent, places = lay_out(parts)
    names = list(sent)

    def body(*refs):
        ins, outs = refs[: len(arrays)], refs[len(arrays) :]
        for late in (True, False):
            for part, (kept, arriving), (kept_at, axis, sent_at) in zip(parts, spots, places):
                half = part.rows // 2
                out, to = (outs[1 + names.index(axis)], sent_at) if late else (outs[0], kept_at)
                skip = half if late else 0
                left = ins[kept[0]].get()[kept[1] + skip : kept[1] + skip + half, :]
                right = ins[arriving[0]].get()[arriving[1] + skip : arriving[1] + skip + half, :]
                out.ref[to : to + half, :] = left + right

    return launched(parts, kernel_call(body, arrays, out_shapes(parts, lanes), tokens=tokens), swap)


def finished(parts):
    arrays, spots = arrays_of(parts)
    lanes = arrays[0].shape[1]

    def body(*refs):
        ins, outs = refs[: len(arrays)], refs[len(arrays) :]
        for part, (kept, arriving), out in zip(parts, spots, outs):
            left = ins[kept[0]].get()[kept[1] : kept[1] + part.rows, :]
            right = ins[arriving[0]].get()[arriving[1] : arriving[1] + part.rows, :]
            out.ref[...] = left.astype(F32) + right.astype(F32)

    return kernel_call(body, arrays, [((part.rows, lanes), F32) for part in parts])


def ffn_grads_kernel(place_ref, keep_in, stack_in, cot_in, stack_mate_in, cot_mate_in, mate_in, *outs, parts, rows):
    at_zero = place_ref[0] == 0
    put = writer(parts, outs)
    lanes = outs[0].ref.shape[1]
    keep, mate = keep_in.get(), mate_in.get()
    half = cot_in.ref.shape[0]
    h3, h3_mate = (ref.get().at[2 * half : 3 * half] for ref in (stack_in, stack_mate_in))
    cot, cot_mate = cot_in.get(), cot_mate_in.get()
    width = cot.shape[1]
    hidden = keep.shape[2]
    for matrix in range(3):
        right, right_mate = (cot, cot_mate) if matrix == 2 else (h3, h3_mate)
        for quarter in range(4):
            units = slice(quarter * hidden // 4, (quarter + 1) * hidden // 4)
            value = dot_tn(keep[matrix, :, units], right[...]) + dot_tn(mate[matrix, :, units], right_mate[...])
            value = value.reshape(hidden // (8 * rows), 2, rows, width)
            low, high = value[:, 0], value[:, 1]
            for far in range(2):
                near = at_zero if far == 0 else jnp.logical_not(at_zero)
                chosen = jnp.where(near, low, high).reshape(hidden // 8, width).astype(BF16)
                index = {"1": quarter // 2, "2": quarter % 2, "x": far}
                for slot in range(width // lanes):
                    at = matrix * (width // lanes) + slot
                    put(at, position(parts[at].axes, index), chosen[:, slot * lanes : (slot + 1) * lanes])


def cross_grads_kernel(
    turn_in, dc_in, stack_in, enc_in, dc_mate_in, stack_mate_in, enc_mate_in, back_in,
    ck_in, ck_far_in, cv_in, cv_far_in, back_mate_in, *outs, parts,
):
    enc_own_out, enc_other_out = outs[-2:]
    put = writer(parts, outs[:-2])
    half = dc_in.ref.shape[0]
    cols = ck_in.ref.shape[1]
    back, length = back_in.get(), 2 * half
    turn = turn_in.get()[...]

    def turned(array):
        return dot(array, turn).astype(BF16)

    dc = [turned(ref.get()[...]) for ref in (dc_in, dc_mate_in)]
    stacks = (stack_in.get(), stack_mate_in.get())
    h2 = [turned(ref[:half, :]) for ref in stacks]
    enc = [turned(ref.get()[...]) for ref in (enc_in, enc_mate_in)]
    first = half
    for out, rows in ((enc_other_out, slice(first + half, first + length)), (enc_own_out, slice(first, first + half))):
        vrows = slice(rows.start + length, rows.stop + length)
        toward = dot_nt(back[rows, :cols], ck_in.get()[...]) + dot_nt(back[rows, cols:], ck_far_in.get()[...])
        toward = toward + dot_nt(back[vrows, :cols], cv_in.get()[...])
        toward = toward + dot_nt(back[vrows, cols:], cv_far_in.get()[...])
        out.ref[...] = toward.astype(out.ref.dtype)
    backs = (back, back_mate_in.get())
    dy = [turned(ref[half + 2 * length :, :]) for ref in backs]
    mixed_two = [ref[half : 2 * half, :] for ref in stacks]
    mixed_one = [ref[3 * half :, :] for ref in stacks]
    dq = [ref[:half, :] for ref in backs]
    dk = [ref[half : half + length, :] for ref in backs]
    dv = [ref[half + length : half + 2 * length, :] for ref in backs]
    for at, (left, right) in enumerate(((dc, mixed_two), (h2, dq), (enc, dk), (enc, dv), (dy, mixed_one))):
        value = (dot_tn(left[0], right[0]) + dot_tn(left[1], right[1])).astype(BF16)
        eighth = value.shape[0] // 4
        for far in range(2):
            for quarter in range(4):
                index = {"1": quarter // 2, "2": quarter % 2, "x": far}
                piece = value[quarter * eighth : (quarter + 1) * eighth, far * cols : (far + 1) * cols]
                put(at, position(parts[at].axes, index), piece)


def self_grads_kernel(turn_in, h1_in, h1_mate_in, grads_in, grads_mate_in, *outs, parts):
    turn = turn_in.get()[...]
    left = dot(h1_in.get()[...], turn).astype(BF16)
    left_mate = dot(h1_mate_in.get()[...], turn).astype(BF16)
    grads, mate = grads_in.get(), grads_mate_in.get()
    _, sent, places = lay_out(parts)
    refs = dict(zip(sent, (out.ref for out in outs[1:])))
    for at, part in enumerate(parts):
        value = (dot_tn(left, grads[at]) + dot_tn(left_mate, mate[at])).astype(BF16)
        half = part.rows // 2
        kept_at, axis, sent_at = places[at]
        quarter = half // 2
        for first in range(2):
            for second in range(2):
                piece = value[(first * 2 + second) * quarter : (first * 2 + second + 1) * quarter]
                index = {"1": first, "2": second}
                major, minor = (index[name] for name in part.axes[:2])
                ref, base = (outs[0].ref, kept_at) if major == 0 else (refs[axis], sent_at)
                ref[base + minor * quarter : base + (minor + 1) * quarter, :] = piece


def turn_kernel(source_in, turn_out):
    size, count = turn_out.ref.shape
    row = lax.broadcasted_iota(jnp.int32, (size, count), 0)
    turn_out.ref[...] = jnp.where(row == source_in.get()[...], 1.0, 0.0).astype(BF16)


def swap_seq(value):
    return lax.ppermute(value, "seq", [(0, 1), (1, 0)])


def swap_dp(value, bit):
    size = lax.axis_size("dp")
    return lax.ppermute(value, "dp", [(i, i ^ (1 << bit)) for i in range(size)])


def swap(value, name):
    return swap_seq(value) if name == "x" else swap_dp(value, int(name))


def local(
    decoder_in,
    encoder_out,
    decoder_segments,
    encoder_segments,
    rel_buckets,
    self_gain,
    self_query,
    self_key,
    self_value,
    self_output,
    bias_table,
    cross_gain,
    cross_query,
    cross_key,
    cross_value,
    cross_output,
    ffn_gain,
    ffn_gate,
    ffn_up,
    ffn_down,
    cotangent,
):
    dp_size = lax.axis_size("dp")
    seq_size = lax.axis_size("seq")
    place = lax.axis_index("seq")
    dp_place = lax.axis_index("dp")
    nbits = dp_size.bit_length() - 1
    late = tuple(str(bit) for bit in range(3, nbits))
    orders = (("x", "1", "2") + late, ("1", "2", "x") + late, ("2", "x", "1") + late)
    half, width = decoder_in.shape
    length = decoder_segments.shape[1]
    heads_here = bias_table.shape[1]
    heads_all = heads_here * seq_size
    buckets_all = bias_table.shape[0]
    cols = self_query.shape[1]
    hidden_dim = ffn_gate.shape[1]
    places = jnp.reshape(place, (1,)).astype(jnp.int32)

    reversed_bits = [
        sum(((at >> (nbits - 1 - bit)) & 1) << bit for bit in range(nbits)) for at in range(dp_size)
    ]
    source_blocks = jnp.array(reversed_bits, jnp.int32) ^ dp_place
    block = width // dp_size
    source = source_blocks[: dp_size // 2, None] * block + jnp.arange(block, dtype=jnp.int32)
    (turn,) = kernel_call(turn_kernel, (source.reshape(1, width // 2),), [((width, width // 2), BF16)])
    ffn_block = hidden_dim // dp_size
    gate_w, up_w, down_w = ffn_gate, ffn_up, ffn_down
    unit_source = source_blocks
    if ffn_block != LANES:
        units = (source_blocks[:, None] * ffn_block + jnp.arange(ffn_block, dtype=jnp.int32)).reshape(-1)
        gate_w, up_w, down_w = (
            jnp.take(ffn_gate, units, axis=1), jnp.take(ffn_up, units, axis=1), jnp.take(ffn_down, units, axis=0)
        )
        unit_source = jnp.arange(hidden_dim // LANES, dtype=jnp.int32)

    decoder_far = swap_seq(decoder_in)
    mine_wide = dp_place & 3
    mine_tall = (dp_place & 1) | ((dp_place >> 1) & 2)
    rows = cols // 4
    wide = jnp.concatenate(
        [lax.dynamic_slice_in_dim(w, mine_wide * rows, rows, 0) for w in (self_output, cross_output)], 0
    )
    rows = width // 4
    tall = jnp.concatenate(
        [
            lax.dynamic_slice_in_dim(w, mine_tall * rows, rows, 0)
            for w in (cross_query, cross_key, cross_value)
        ],
        1,
    )
    wide = swap_seq(wide)
    tall = swap_seq(tall)
    wide_next, tall_next = swap_dp(wide, 1), swap_dp(tall, 2)
    wide_parts = (wide, swap_dp(wide, 0), wide_next, swap_dp(wide_next, 0))
    tall_parts = (tall, swap_dp(tall, 0), tall_next, swap_dp(tall_next, 0))
    encoder_far = swap_seq(encoder_out)
    cot_mate = swap_dp(cotangent, 0)

    span = length + LANES
    near = length - BLOCK
    line_buckets = jnp.concatenate(
        [
            rel_buckets[: near + 1][::-1],
            jnp.full((span - length,), -1, jnp.int32),
            rel_buckets[near + 1 :][::-1],
        ]
    )
    onehot = (
        line_buckets[:, None] == jnp.arange(buckets_all, dtype=jnp.int32)[None, :]
    ).astype(F32)
    line = jnp.einsum("bh,tb->ht", bias_table, onehot, precision=HIGH)
    (strip,) = kernel_call(strip_kernel, (line,), [((heads_here, BLOCK, length), F32)])

    segc = decoder_segments.reshape(length, 1)
    dseg = lax.dynamic_slice_in_dim(segc, place * half, half, 0)
    eseg = jnp.where(
        place == 0, encoder_segments, jnp.concatenate([encoder_segments[:, half:], encoder_segments[:, :half]], 1)
    )
    self_row, cross_row, ffn_row = (gain.reshape(1, width) for gain in (self_gain, cross_gain, ffn_gain))
    quarters = jnp.stack([mine_wide, mine_tall]).astype(jnp.int32)

    tokens = ((half, cols), BF16)
    mixed_own, mixed_other, h1, q1, k1, v1, p1 = kernel_call(
        self_forward_kernel,
        (
            places, decoder_in, self_row, self_query, decoder_far,
            self_key, self_value, segc, decoder_segments, strip,
        ),
        [
            tokens, tokens, ((length, width), BF16),
            ((length, cols), BF16), ((length, cols), BF16), ((length, cols), BF16),
            ((heads_here, length, length), BF16),
        ],
        scratch=(pltpu.VMEM((length, cols), BF16),),
        scalars=1,
        flops=2 * length * width * cols * 3 + 4 * length * length * cols,
        tokens=(turn, dseg, eseg, cross_row, ffn_row, quarters, onehot, unit_source),
    )
    mixed_far = swap_seq(mixed_other)
    h1_mate = swap_dp(h1, 0)

    so_far, co_far, cq_far, ck_far, cv_far, k2, v2, encoder_full = kernel_call(
        unpack_kernel,
        (
            quarters, *wide_parts, *tall_parts,
            encoder_out, encoder_far, cross_key, cross_value,
        ),
        [((cols, width), BF16)] * 2 + [((width, cols), BF16)] * 3 + [((length, width), BF16)] * 3,
        scalars=1,
        flops=4 * length * width * width,
    )
    encoder_mate = swap_dp(encoder_full, 0)
    x_two, stack, q2, p2, x_three = kernel_call(
        middle_kernel,
        (
            decoder_in, mixed_own, self_output, mixed_far, so_far, cross_row, cross_query, cq_far,
            k2, v2, dseg, eseg, cross_output, co_far, ffn_row,
        ),
        [
            ((half, width), F32), ((4 * half, width), BF16), ((half, width), BF16),
            ((heads_all, half, length), BF16), ((half, width), F32),
        ],
        flops=4 * half * length * width + 6 * half * width * width,
    )
    stack_mate = swap_dp(stack, 0)
    layer_out, ffn_keep, ffn_send, grad_x_three, dc, do2, gain_three = ffn_call(
        unit_source, x_three, stack, cotangent, gate_w, up_w, down_w, ffn_row, cross_output, co_far
    )

    ffn_mate = swap_dp(ffn_send, 0)
    dc_mate = swap_dp(dc, 0)
    ffn_parts = [Part(hidden_dim // 2, order) for order in orders for _ in range(width // cols)]
    ffn_parts = launched(
        ffn_parts,
        kernel_call(
            functools.partial(ffn_grads_kernel, parts=ffn_parts, rows=ffn_block // seq_size),
            (places, ffn_keep, stack, cotangent, stack_mate, cot_mate, ffn_mate),
            out_shapes(ffn_parts, cols),
            scalars=1,
            flops=6 * half * hidden_dim * width,
        ),
        swap,
    )

    back, grad_x_two, do1_own, do1_other, gain_two = kernel_call(
        cross_backward_kernel,
        (
            do2, q2, k2, v2, p2, cross_query, cq_far, x_two, cross_row, grad_x_three, self_output, so_far,
        ),
        [((2 * half + 2 * length, width), BF16), ((half, width), F32), tokens, tokens, ((1, width), F32)],
        scratch=(
            pltpu.VMEM((length, LANES), F32), pltpu.VMEM((length, LANES), F32),
        ),
        flops=8 * half * length * width + 4 * half * width * width,
        tokens=[ffn_parts[0].kept[0]],
    )
    do1_far = swap_seq(do1_other)
    back_mate = swap_dp(back, 0)
    ffn_parts = stepped(ffn_parts, swap, tokens=(back,))
    axes = (orders[0], orders[0], orders[1], orders[1], orders[2])
    cross_parts = [Part(width, order) for order in axes]
    results = kernel_call(
        functools.partial(cross_grads_kernel, parts=cross_parts),
        (
            turn, dc, stack, encoder_full, dc_mate, stack_mate, encoder_mate, back,
            cross_key, ck_far, cross_value, cv_far, back_mate,
        ),
        out_shapes(cross_parts, cols) + [((half, width), F32), ((half, width), BF16)],
        flops=2 * width * width * (half * 3 + length * 4),
        tokens=(ffn_parts[0].kept[0],),
    )
    encoder_own, encoder_other = results[-2:]
    cross_parts = launched(cross_parts, results[:-2], swap)

    self_grads, line_grads, h1_own, h1_other, gain_one = kernel_call(
        self_backward_kernel,
        (
            places, q1, k1, v1, do1_own, do1_far, p1, self_query, self_key, self_value, decoder_in, decoder_far,
        ),
        [
            ((3, length, cols), BF16), ((heads_here, 1, span), F32), ((half, width), F32),
            ((half, width), BF16), ((1, width), F32),
        ],
        scratch=(
            pltpu.VMEM((length, cols), BF16), pltpu.VMEM((length, LANES), F32),
            pltpu.VMEM((length, LANES), F32), pltpu.VMEM((2, BLOCK, span), F32),
        ),
        scalars=1,
        flops=8 * length * length * cols + 6 * length * width * cols,
        tokens=(cross_parts[0].kept[0],),
    )
    self_mate = swap_dp(self_grads, 0)
    h1_far = swap_seq(h1_other)
    ffn_parts = stepped(ffn_parts, swap, tokens=(self_grads,))
    self_parts = [Part(width // 2, order) for order in (("1", "2") + late, ("2", "1") + late, ("1", "2") + late)]
    self_parts = launched(
        self_parts,
        kernel_call(
            functools.partial(self_grads_kernel, parts=self_parts),
            (turn, h1, h1_mate, self_grads, self_mate),
            out_shapes(self_parts, cols),
            flops=6 * length * width * cols,
            tokens=(ffn_parts[0].kept[0],),
        ),
        swap,
    )
    encoder_far_grads = swap_seq(encoder_other)

    table_local = jnp.einsum("ht,tb->bh", line_grads[:, 0, :], onehot, precision=HIGH)
    table_full = lax.dynamic_update_slice(
        jnp.zeros((buckets_all, heads_all), F32), table_local, (0, place * heads_here)
    )
    small = jnp.concatenate([gain_one[0], gain_two[0], gain_three[0], table_full.reshape(-1)])
    small = small.reshape(-1, LANES)
    small = small + swap_seq(small)
    for bit in range(nbits):
        small = small + swap_dp(small, bit)
    small = small.reshape(-1)
    gain_one, gain_two, gain_three = small[:width], small[width : 2 * width], small[2 * width : 3 * width]
    table_sum = small[3 * width :].reshape(buckets_all, heads_all)

    cross_parts = stepped(cross_parts, swap, tokens=(self_parts[0].kept[0],))
    parts = self_parts + cross_parts + ffn_parts
    order = list(range(len(parts)))
    finals = [None] * len(parts)
    while parts:
        over = [at for at, part in enumerate(parts) if not part.axes]
        if over:
            for at, value in zip(over, finished([parts[at] for at in over])):
                finals[order[at]] = value
        going = [at for at in range(len(parts)) if at not in over]
        order = [order[at] for at in going]
        parts = [parts[at] for at in going]
        if parts:
            parts = stepped(parts, swap)
    sum_q, sum_k, sum_v, sum_co, sum_cq, sum_ck, sum_cv, sum_so = finals[:8]
    rest = [jnp.concatenate(finals[at : at + width // cols], axis=1) for at in range(8, len(finals), width // cols)]
    ffn_sums = (rest[0].T, rest[1].T, rest[2])
    grad_encoder = encoder_own + encoder_far_grads.astype(F32)
    grad_h1 = h1_own + h1_far.astype(F32)
    toward, _ = normed_back(decoder_in.astype(F32), self_row, grad_h1)
    grad_decoder = grad_x_two + toward
    return (
        layer_out, grad_decoder, grad_encoder, gain_one, sum_q, sum_k, sum_v, sum_so.T, table_sum,
        gain_two, sum_cq, sum_ck, sum_cv, sum_co.T, gain_three, *ffn_sums,
    )


def solution(mesh):
    tokens, both = P(("dp", "seq"), None), P("dp", "seq")
    col, row = P(None, "seq"), P("seq", None)
    return jax.shard_map(
        local,
        mesh=mesh,
        in_specs=(
            tokens, tokens, P("dp", None), P("dp", None), P(), P(), col, col, col, row, col,
            P(), col, col, col, row, P(), P(), P(), P(), tokens,
        ),
        out_specs=(
            tokens, tokens, tokens, P(), both, both, both, P("seq", "dp"), P(), P(), both, both,
            both, P("seq", "dp"), P(), P(None, ("dp", "seq")), P(None, ("dp", "seq")), tokens,
        ),
        check_vma=False,
    )
```
